32 devices in a mesh: groups: 2 (over x), lbond: 16 (over z, y, core).
Axes of the slice: x: 2, y: 2, z: 4, core: 2. Of those that a mesh axis runs over, the one named last changes fastest.
Arguments:
- env_in: bfloat16 [4096, 1024], P('lbond', 'groups'), parts along dimension 1, may hold values from -6 to 6
- site_tensors: bfloat16 [4, 4096, 4, 4096], P(None, 'lbond'), may hold values from -0.125 to 0.125
- weight_table: float32 [64, 4], replicated, may hold values from -3 to 3
- state_codes: int32 [4, 1024], P(None, 'groups'), parts along dimension 1, may hold values from 0 to 63
- rescale: int32 [4], replicated, may hold values from 1 to 3
Outputs:
- env_out: bfloat16 [4096, 1024], P('lbond', 'groups'), parts along dimension 1
The draws below stay inside these ranges and needn't reach their ends.
There are 2 independent parts, one for each index of `groups`. The reference program is written for one: setup_inputs(seed, part) draws one part's arguments, and reference() takes and returns one part's arrays. A program takes and returns all parts, laid end to end along the dimension named above; an argument that names none is the same for every part. Nothing has to cross between parts.
All inputs are finite; a program needn't handle non-finite values.
Results may differ from the reference program's by a relative error of at most 0.018.
Values may be sent and summed in bfloat16 or wider, within the bound.
A program may use at most 128 MiB of HBM per device.

```python
import jax
import jax.numpy as jnp

CHI = 4096
PHOT = 4
SITES = 4
TABLE = 64
ROWS = 512


def set_ends(array, key, low, top_value):
    shape = array.shape
    index_at = [jax.random.randint(jax.random.fold_in(key, axis), (), 0, shape[axis]) for axis in range(len(shape))]
    array = array.at[tuple(index_at)].set(low)
    longest = shape.index(max(shape))
    index_at[longest] = (index_at[longest] + 1) % shape[longest]
    return array.at[tuple(index_at)].set(top_value)


def with_spikes(result, key, source, target, shards_of, factor):
    owner, partner = [(jnp.arange(result.shape[axis_at]) // (result.shape[axis_at] // shards_of)).reshape([-1 if axis == axis_at else 1 for axis in range(result.ndim)]) for axis_at in (source, target)]
    chosen = jax.random.permutation(key, shards_of)[partner]
    strong = (owner == chosen) | (owner == (partner + shards_of // 2) % shards_of)
    return jnp.where(strong, factor * result, result)


def block_scale(stream_key, shape, split, smallest, top_value):
    gain = 1.0
    for axis_at, shards_of in split:
        draws = jax.random.uniform(jax.random.fold_in(jax.random.fold_in(stream_key, 6), axis_at), (shards_of,), jnp.float32, smallest / len(split), top_value / len(split))
        gain = gain * jnp.repeat(jnp.exp(draws), shape[axis_at] // shards_of).reshape((-1,) + (1,) * (len(shape) - 1 - axis_at))
    return gain


def noise(key, shape, scale, bound, pieces=(), held_as=jnp.bfloat16):
    entries = jax.random.normal(key, shape, jnp.float32) * scale
    if len(pieces) > 0:
        entries = block_scale(key, shape, pieces, -0.22, 0.18) * entries
    return jnp.clip(entries, min=-bound, max=bound).astype(held_as)


def noise_with(key, shape, width, reach, split, heavy, dtype=jnp.bfloat16):
    array = width * jax.random.normal(key, shape, jnp.float32)
    if split:
        array = array * block_scale(key, shape, split, -0.22, 0.18)
    return jnp.clip(with_spikes(array, jax.random.fold_in(key, 3), *heavy), -reach, reach).astype(dtype)


def setup_inputs(seed: int = 0, part: int = 0) -> dict:
    seeds = jax.random.split(jax.random.key(seed), 6)
    part_splits = jax.random.split(jax.random.fold_in(seeds[5], part), 6)
    env_in = noise(part_splits[0], (CHI, ROWS), 1.0, 6.0, ((0, 16),))
    site_tensors = noise_with(seeds[1], (SITES, CHI, PHOT, CHI), CHI ** -0.5, 0.125, ((1, 16),), (1, 3, 16, 2.0))
    weight_table = noise(seeds[2], (TABLE, PHOT), 0.5, 3.0, (), jnp.float32)
    state_codes = set_ends(jax.random.randint(part_splits[3], (SITES, ROWS), 0, TABLE), jax.random.fold_in(part_splits[3], 1), 0, TABLE - 1).astype(jnp.int32)
    rescale = set_ends(jax.random.randint(seeds[4], (SITES,), 1, 4), jax.random.fold_in(seeds[4], 1), 1, 3).astype(jnp.int32)
    return {"env_in": env_in, "site_tensors": site_tensors, "weight_table": weight_table, "state_codes": state_codes, "rescale": rescale}


def reference(env_in, site_tensors, weight_table, state_codes, rescale):
    weights = weight_table[state_codes]
    env = env_in
    for index in range(SITES):
        mix = jnp.transpose(weights[index])
        scaled = (env.astype(jnp.float32)[:, None, :] * mix[None, :, :]).astype(jnp.bfloat16)
        scaled = scaled.reshape(CHI * PHOT, ROWS)
        flat = site_tensors[index].reshape(CHI * PHOT, CHI)
        product = jnp.dot(flat.T, scaled, preferred_element_type=jnp.float32)
        factor = rescale[index].astype(jnp.float32) * 0.5
        env = (product * factor).astype(jnp.bfloat16)
    return env
```

```python
import functools

import jax
import jax.numpy as jnp
from jax import lax
from jax.experimental import pallas as pl
from jax.experimental.pallas import tpu as pltpu
from jax.sharding import PartitionSpec as P

CHUNKS = 2
LAG = 2
RING = 4
LANES = 128


def kernel(
    wide, tall, rescale_ref, env_ref, weight_ref, tensor_ref, out_ref,
    raw, packed, spread, scaled, send_a, recv_a, keep_a, send_b, recv_b, keep_b,
    send_z, recv_z, keep_z, raw_sem, sa_sem, ra_sem, sb_sem, rb_sem, sz_sem, rz_sem,
):
    sites, local, photon, _ = tensor_ref.shape
    rows = env_ref.shape[0] // CHUNKS
    depth = local * photon
    pieces = sites * CHUNKS * tall
    me = lax.axis_index("lbond")
    core = lax.rem(me, 2)
    chip = lax.div(me, 2)
    y = lax.rem(chip, wide)
    z = lax.div(chip, wide)
    mate = me + 1 - 2 * core
    across = (z * wide + (wide - 1 - y)) * 2 + core

    def at_z(other):
        return (other * wide + y) * 2 + core

    def target(q):
        return lax.rem(z + 1 + q, tall)

    barrier = pltpu.get_barrier_semaphore()
    peers = [mate] + ([across] if wide > 1 else [])
    peers += [at_z(target(q)) for q in range(tall - 1)]
    for peer in peers:
        pl.semaphore_signal(barrier, inc=1, device_id={"lbond": peer}, device_id_type=pl.DeviceIdType.MESH)

    def fetch(n):
        site = lax.div(n, tall)
        goal = target(lax.rem(n, tall))
        width = raw.shape[-1]
        columns = pl.ds(pl.multiple_of(goal * width, LANES), width)
        slot = lax.rem(n, 2)
        return pltpu.make_async_copy(tensor_ref.at[site, :, :, columns], raw.at[slot], raw_sem.at[slot])

    for n in range(2):
        fetch(jnp.int32(n)).start()

    left = lax.broadcasted_iota(jnp.int32, (local, depth), 0)
    flat = lax.broadcasted_iota(jnp.int32, (local, depth), 1)
    spread[...] = jnp.where(
        (flat >= left * photon) & (flat < left * photon + photon), 1.0, 0.0
    ).astype(jnp.bfloat16)

    def scale_rows(env, site, c):
        mix = weight_ref[site, pl.ds(pl.multiple_of(c * rows, rows), rows), :]
        for k in range(0, depth, LANES):
            piece = jnp.dot(env, spread[:, k : k + LANES], preferred_element_type=jnp.float32)
            scaled[c, :, k : k + LANES] = (piece * mix).astype(jnp.bfloat16)

    for c in range(CHUNKS):
        scale_rows(env_ref[c * rows : (c + 1) * rows, :], 0, c)

    def split(t):
        unit = lax.div(t, tall)
        return lax.div(unit, CHUNKS), lax.rem(unit, CHUNKS), lax.rem(t, tall)

    def to_mate(t):
        slot = lax.rem(t, RING)
        return pltpu.make_async_remote_copy(
            send_a.at[slot], recv_a.at[slot], sa_sem.at[slot], ra_sem.at[slot],
            device_id={"lbond": mate}, device_id_type=pl.DeviceIdType.MESH,
        )

    def to_across(t):
        slot = lax.rem(t, RING)
        return pltpu.make_async_remote_copy(
            send_b.at[slot], recv_b.at[slot], sb_sem.at[slot], rb_sem.at[slot],
            device_id={"lbond": across}, device_id_type=pl.DeviceIdType.MESH,
        )

    def to_owner(site, c, q):
        half = lax.rem(site, 2)
        return pltpu.make_async_remote_copy(
            send_z.at[half, c, q], recv_z.at[half, c, q], sz_sem.at[half, c, q], rz_sem.at[half, c, q],
            device_id={"lbond": at_z(target(q))}, device_id_type=pl.DeviceIdType.MESH,
        )

    pl.semaphore_wait(barrier, len(peers))

    def step(t, carry):
        @pl.when(t < pieces)
        def _():
            site, c, q = split(t)
            goal = target(q)

            @pl.when(c == 0)
            def _():
                n = site * tall + q
                slot = lax.rem(n, 2)
                fetch(n).wait()
                width = packed.shape[-1]
                for b in range(2 * wide):
                    for k in range(0, local, 16):
                        block = raw[slot, k : k + 16, :, b * width : (b + 1) * width]
                        packed[goal, b, k * photon : (k + 16) * photon, :] = block.reshape(16 * photon, width)

                @pl.when(n + 2 < sites * tall)
                def _():
                    fetch(n + 2).start()

            slot = lax.rem(t, RING)
            for b in range(wide):
                send_a[slot, b] = jnp.dot(
                    scaled[c], packed[goal, 2 * b + 1 - core], preferred_element_type=jnp.float32
                ).astype(jnp.bfloat16)
            to_mate(t).start()
            for b in range(wide):
                keep_a[lax.rem(t, 2), b] = jnp.dot(
                    scaled[c], packed[goal, 2 * b + core], preferred_element_type=jnp.float32
                )

        @pl.when((t >= 1) & (t < pieces + 1))
        def _():
            u = t - 1
            slot = lax.rem(u, RING)
            half = lax.rem(u, 2)
            to_mate(u).wait()
            if wide > 1:
                far = wide - 1 - y
                send_b[slot] = (keep_a[half, far] + recv_a[slot, far].astype(jnp.float32)).astype(jnp.bfloat16)
                to_across(u).start()
            keep_b[half] = keep_a[half, y] + recv_a[slot, y].astype(jnp.float32)

        @pl.when((t >= 2) & (t < pieces + 2))
        def _():
            u = t - 2
            site, c, q = split(u)
            total = keep_b[lax.rem(u, 2)]
            if wide > 1:
                to_across(u).wait()
                total = total + recv_b[lax.rem(u, RING)].astype(jnp.float32)

            @pl.when(q < tall - 1)
            def _():
                send_z[lax.rem(site, 2), c, q] = total.astype(jnp.bfloat16)
                to_owner(site, c, q).start()

            @pl.when(q == tall - 1)
            def _():
                keep_z[c] = total

        last = t - 2 - LAG

        @pl.when((last >= 0) & (lax.rem(last + 1, tall) == 0))
        def _():
            site, c, _ = split(last)
            total = keep_z[c]
            for q in range(tall - 1):
                to_owner(site, c, q).wait()
                total = total + recv_z[lax.rem(site, 2), c, q].astype(jnp.float32)
            env = (total * (rescale_ref[site].astype(jnp.float32) * 0.5)).astype(jnp.bfloat16)

            @pl.when(site < sites - 1)
            def _():
                scale_rows(env, site + 1, c)

            @pl.when(site == sites - 1)
            def _():
                out_ref[pl.ds(pl.multiple_of(c * rows, rows), rows), :] = env

        return carry

    lax.fori_loop(0, pieces + 2 + LAG, step, 0)


def on_device(wide, tall, env_in, site_tensors, weight_table, state_codes, rescale):
    sites, local, photon, right = site_tensors.shape
    entries = weight_table.shape[0]
    rows = env_in.shape[1] // CHUNKS
    depth = local * photon
    matches = (
        state_codes[:, :, None] == jnp.arange(entries, dtype=jnp.int32)[None, None, :]
    ).astype(jnp.float32)
    table = jnp.tile(weight_table, (1, LANES // photon))
    weights = jnp.einsum("srt,tl->srl", matches, table, precision=lax.Precision.HIGHEST)
    vmem = pl.BlockSpec(memory_space=pltpu.VMEM)
    half, full = jnp.bfloat16, jnp.float32
    dma = pltpu.SemaphoreType.DMA
    out = pl.pallas_call(
        functools.partial(kernel, wide, tall),
        out_shape=jax.ShapeDtypeStruct((env_in.shape[1], local), half),
        in_specs=[pl.BlockSpec(memory_space=pltpu.SMEM), vmem, vmem, pl.BlockSpec(memory_space=pl.ANY)],
        out_specs=vmem,
        scratch_shapes=[
            pltpu.VMEM((2, local, photon, right // tall), half),
            pltpu.VMEM((tall, 2 * wide, depth, local), half),
            pltpu.VMEM((local, depth), half),
            pltpu.VMEM((CHUNKS, rows, depth), half),
            pltpu.VMEM((RING, wide, rows, local), half),
            pltpu.VMEM((RING, wide, rows, local), half),
            pltpu.VMEM((2, wide, rows, local), full),
            pltpu.VMEM((RING, rows, local), half),
            pltpu.VMEM((RING, rows, local), half),
            pltpu.VMEM((2, rows, local), full),
            pltpu.VMEM((2, CHUNKS, tall - 1, rows, local), half),
            pltpu.VMEM((2, CHUNKS, tall - 1, rows, local), half),
            pltpu.VMEM((CHUNKS, rows, local), full),
            dma((2,)),
            dma((RING,)),
            dma((RING,)),
            dma((RING,)),
            dma((RING,)),
            dma((2, CHUNKS, tall - 1)),
            dma((2, CHUNKS, tall - 1)),
        ],
        compiler_params=pltpu.CompilerParams(
            collective_id=0, has_side_effects=True, vmem_limit_bytes=60 * 1024 * 1024
        ),
    )(rescale, env_in.T, weights, site_tensors)
    return out.T


def solution(mesh):
    wide = max(1, 4 // mesh.shape["groups"])
    tall = mesh.shape["lbond"] // (2 * wide)
    placed = (P("lbond", "groups"), P(None, "lbond", None, None), P(), P(None, "groups"), P())
    return jax.shard_map(
        functools.partial(on_device, wide, tall),
        mesh=mesh, in_specs=placed, out_specs=P("lbond", "groups"), check_vma=False,
    )
```

```python
import functools

import jax
import jax.numpy as jnp
from jax import lax
from jax.experimental import pallas as pl
from jax.experimental.pallas import tpu as pltpu
from jax.sharding import PartitionSpec as P

CHUNKS = 2
LAG = 1
HOLD = 3
RING = 4
RING_B = 2 * HOLD
LANES = 128


def kernel(
    wide, tall, rescale_ref, env_ref, weight_ref, tensor_ref, out_ref,
    raw, packed, spread, scaled, send_a, recv_a, keep_a, send_b, recv_b, keep_b,
    send_z, recv_z, keep_z, raw_sem, sa_sem, ra_sem, sb_sem, rb_sem, sz_sem, rz_sem,
):
    sites, local, photon, _ = tensor_ref.shape
    rows = env_ref.shape[0] // CHUNKS
    depth = local * photon
    pieces = sites * CHUNKS * tall
    me = lax.axis_index("lbond")
    core = lax.rem(me, 2)
    chip = lax.div(me, 2)
    y = lax.rem(chip, wide)
    z = lax.div(chip, wide)
    mate = me + 1 - 2 * core
    across = (z * wide + (wide - 1 - y)) * 2 + core

    def at_z(other):
        return (other * wide + y) * 2 + core

    def target(q):
        return lax.rem(z + 1 + q, tall)

    barrier = pltpu.get_barrier_semaphore()
    peers = [mate] + ([across] if wide > 1 else [])
    peers += [at_z(target(q)) for q in range(tall - 1)]
    for peer in peers:
        pl.semaphore_signal(barrier, inc=1, device_id={"lbond": peer}, device_id_type=pl.DeviceIdType.MESH)

    def fetch(n):
        site = lax.div(n, tall)
        goal = target(lax.rem(n, tall))
        width = raw.shape[-1]
        columns = pl.ds(pl.multiple_of(goal * width, LANES), width)
        slot = lax.rem(n, 2)
        return pltpu.make_async_copy(tensor_ref.at[site, :, :, columns], raw.at[slot], raw_sem.at[slot])

    for n in range(2):
        fetch(jnp.int32(n)).start()

    left = lax.broadcasted_iota(jnp.int32, (local, depth), 0)
    flat = lax.broadcasted_iota(jnp.int32, (local, depth), 1)
    spread[...] = jnp.where(
        (flat >= left * photon) & (flat < left * photon + photon), 1.0, 0.0
    ).astype(jnp.bfloat16)

    def scale_rows(env, site, c):
        mix = weight_ref[site, pl.ds(pl.multiple_of(c * rows, rows), rows), :]
        for k in range(0, depth, LANES):
            piece = jnp.dot(env, spread[:, k : k + LANES], preferred_element_type=jnp.float32)
            scaled[c, :, k : k + LANES] = (piece * mix).astype(jnp.bfloat16)

    for c in range(CHUNKS):
        scale_rows(env_ref[c * rows : (c + 1) * rows, :], 0, c)

    def split(t):
        unit = lax.div(t, tall)
        return lax.div(unit, CHUNKS), lax.rem(unit, CHUNKS), lax.rem(t, tall)

    def to_mate(t):
        slot = lax.rem(t, RING)
        return pltpu.make_async_remote_copy(
            send_a.at[slot], recv_a.at[slot], sa_sem.at[slot], ra_sem.at[slot],
            device_id={"lbond": mate}, device_id_type=pl.DeviceIdType.MESH,
        )

    def to_across(t):
        slot = lax.rem(t, RING_B)
        return pltpu.make_async_remote_copy(
            send_b.at[slot], recv_b.at[slot], sb_sem.at[slot], rb_sem.at[slot],
            device_id={"lbond": across}, device_id_type=pl.DeviceIdType.MESH,
        )

    def to_owner(site, c, q):
        half = lax.rem(site, 2)
        return pltpu.make_async_remote_copy(
            send_z.at[half, c, q], recv_z.at[half, c, q], sz_sem.at[half, c, q], rz_sem.at[half, c, q],
            device_id={"lbond": at_z(target(q))}, device_id_type=pl.DeviceIdType.MESH,
        )

    pl.semaphore_wait(barrier, len(peers))

    def step(t, carry):
        @pl.when(t < pieces)
        def _():
            site, c, q = split(t)
            goal = target(q)

            @pl.when(c == 0)
            def _():
                n = site * tall + q
                slot = lax.rem(n, 2)
                fetch(n).wait()
                width = packed.shape[-1]
                for b in range(2 * wide):
                    for k in range(0, local, 16):
                        block = raw[slot, k : k + 16, :, b * width : (b + 1) * width]
                        packed[goal, b, k * photon : (k + 16) * photon, :] = block.reshape(16 * photon, width)

                @pl.when(n + 2 < sites * tall)
                def _():
                    fetch(n + 2).start()

            slot = lax.rem(t, RING)
            for b in range(wide):
                send_a[slot, b] = jnp.dot(
                    scaled[c], packed[goal, 2 * b + 1 - core], preferred_element_type=jnp.float32
                ).astype(jnp.bfloat16)
            to_mate(t).start()
            for b in range(wide):
                keep_a[lax.rem(t, 2), b] = jnp.dot(
                    scaled[c], packed[goal, 2 * b + core], preferred_element_type=jnp.float32
                )

        @pl.when((t >= 1) & (t < pieces + 1))
        def _():
            u = t - 1
            slot = lax.rem(u, RING)
            half = lax.rem(u, 2)
            to_mate(u).wait()
            if wide > 1:
                far = wide - 1 - y
                send_b[lax.rem(u, RING_B)] = (keep_a[half, far] + recv_a[slot, far].astype(jnp.float32)).astype(jnp.bfloat16)
                to_across(u).start()
            keep_b[lax.rem(u, HOLD)] = keep_a[half, y] + recv_a[slot, y].astype(jnp.float32)

        @pl.when((t >= HOLD) & (t < pieces + HOLD))
        def _():
            u = t - HOLD
            site, c, q = split(u)
            total = keep_b[lax.rem(u, HOLD)]
            if wide > 1:
                to_across(u).wait()
                total = total + recv_b[lax.rem(u, RING_B)].astype(jnp.float32)

            @pl.when(q < tall - 1)
            def _():
                send_z[lax.rem(site, 2), c, q] = total.astype(jnp.bfloat16)
                to_owner(site, c, q).start()

            @pl.when(q == tall - 1)
            def _():
                keep_z[c] = total

        last = t - HOLD - LAG

        @pl.when((last >= 0) & (lax.rem(last + 1, tall) == 0))
        def _():
            site, c, _ = split(last)
            total = keep_z[c]
            for q in range(tall - 1):
                to_owner(site, c, q).wait()
                total = total + recv_z[lax.rem(site, 2), c, q].astype(jnp.float32)
            env = (total * (rescale_ref[site].astype(jnp.float32) * 0.5)).astype(jnp.bfloat16)

            @pl.when(site < sites - 1)
            def _():
                scale_rows(env, site + 1, c)

            @pl.when(site == sites - 1)
            def _():
                out_ref[pl.ds(pl.multiple_of(c * rows, rows), rows), :] = env

        return carry

    lax.fori_loop(0, pieces + HOLD + LAG, step, 0)


def on_device(wide, tall, env_in, site_tensors, weight_table, state_codes, rescale):
    sites, local, photon, right = site_tensors.shape
    entries = weight_table.shape[0]
    rows = env_in.shape[1] // CHUNKS
    depth = local * photon
    matches = (
        state_codes[:, :, None] == jnp.arange(entries, dtype=jnp.int32)[None, None, :]
    ).astype(jnp.float32)
    table = jnp.tile(weight_table, (1, LANES // photon))
    weights = jnp.einsum("srt,tl->srl", matches, table, precision=lax.Precision.HIGHEST)
    vmem = pl.BlockSpec(memory_space=pltpu.VMEM)
    half, full = jnp.bfloat16, jnp.float32
    dma = pltpu.SemaphoreType.DMA
    out = pl.pallas_call(
        functools.partial(kernel, wide, tall),
        out_shape=jax.ShapeDtypeStruct((env_in.shape[1], local), half),
        in_specs=[pl.BlockSpec(memory_space=pltpu.SMEM), vmem, vmem, pl.BlockSpec(memory_space=pl.ANY)],
        out_specs=vmem,
        scratch_shapes=[
            pltpu.VMEM((2, local, photon, right // tall), half),
            pltpu.VMEM((tall, 2 * wide, depth, local), half),
            pltpu.VMEM((local, depth), half),
            pltpu.VMEM((CHUNKS, rows, depth), half),
            pltpu.VMEM((RING, wide, rows, local), half),
            pltpu.VMEM((RING, wide, rows, local), half),
            pltpu.VMEM((2, wide, rows, local), full),
            pltpu.VMEM((RING_B, rows, local), half),
            pltpu.VMEM((RING_B, rows, local), half),
            pltpu.VMEM((HOLD, rows, local), full),
            pltpu.VMEM((2, CHUNKS, tall - 1, rows, local), half),
            pltpu.VMEM((2, CHUNKS, tall - 1, rows, local), half),
            pltpu.VMEM((CHUNKS, rows, local), full),
            dma((2,)),
            dma((RING,)),
            dma((RING,)),
            dma((RING_B,)),
            dma((RING_B,)),
            dma((2, CHUNKS, tall - 1)),
            dma((2, CHUNKS, tall - 1)),
        ],
        compiler_params=pltpu.CompilerParams(
            collective_id=0, has_side_effects=True, vmem_limit_bytes=60 * 1024 * 1024
        ),
    )(rescale, env_in.T, weights, site_tensors)
    return out.T


def solution(mesh):
    wide = max(1, 4 // mesh.shape["groups"])
    tall = mesh.shape["lbond"] // (2 * wide)
    placed = (P("lbond", "groups"), P(None, "lbond", None, None), P(), P(None, "groups"), P())
    return jax.shard_map(
        functools.partial(on_device, wide, tall),
        mesh=mesh, in_specs=placed, out_specs=P("lbond", "groups"), check_vma=False,
    )
```

```python
import functools

import jax
import jax.numpy as jnp
from jax import lax
from jax.experimental import pallas as pl
from jax.experimental.pallas import tpu as pltpu
from jax.sharding import PartitionSpec as P

CHUNKS = 2
LAG = 1
HOLD = 3
RING = 4
RING_B = 2 * HOLD
LANES = 128


def kernel(
    wide, tall, rescale_ref, env_ref, code_ref, table_ref, tensor_ref, out_ref,
    raw, packed, spread, scaled, send_a, recv_a, keep_a, send_b, recv_b, keep_b,
    send_z, recv_z, keep_z, raw_sem, sa_sem, ra_sem, sb_sem, rb_sem, sz_sem, rz_sem,
):
    sites, local, photon, _ = tensor_ref.shape
    rows = env_ref.shape[1] // CHUNKS
    depth = local * photon
    pieces = sites * CHUNKS * tall
    me = lax.axis_index("lbond")
    core = lax.rem(me, 2)
    chip = lax.div(me, 2)
    y = lax.rem(chip, wide)
    z = lax.div(chip, wide)
    mate = me + 1 - 2 * core
    across = (z * wide + (wide - 1 - y)) * 2 + core

    def at_z(other):
        return (other * wide + y) * 2 + core

    def target(q):
        return lax.rem(z + 1 + q, tall)

    barrier = pltpu.get_barrier_semaphore()
    peers = [mate] + ([across] if wide > 1 else [])
    peers += [at_z(target(q)) for q in range(tall - 1)]
    for peer in peers:
        pl.semaphore_signal(barrier, inc=1, device_id={"lbond": peer}, device_id_type=pl.DeviceIdType.MESH)

    def fetch(n):
        site = lax.div(n, tall)
        goal = target(lax.rem(n, tall))
        width = raw.shape[-1]
        columns = pl.ds(pl.multiple_of(goal * width, LANES), width)
        slot = lax.rem(n, 2)
        return pltpu.make_async_copy(tensor_ref.at[site, :, :, columns], raw.at[slot], raw_sem.at[slot])

    for n in range(2):
        fetch(jnp.int32(n)).start()

    left = lax.broadcasted_iota(jnp.int32, (local, depth), 0)
    flat = lax.broadcasted_iota(jnp.int32, (local, depth), 1)
    spread[...] = jnp.where(
        (flat >= left * photon) & (flat < left * photon + photon), 1.0, 0.0
    ).astype(jnp.bfloat16)

    def scale_rows(env, flip, site, c):
        codes = code_ref[pl.ds(site, 1), pl.ds(pl.multiple_of(c * rows, rows), rows)]
        entries = table_ref.shape[0]
        index = lax.broadcasted_iota(jnp.int32, (entries, rows), 0)
        match = jnp.where(index == codes, 1.0, 0.0).astype(jnp.bfloat16)
        mix = jnp.zeros((rows, LANES), jnp.float32)
        rest = table_ref[...]
        terms = []
        for _ in range(3):
            term = rest.astype(jnp.bfloat16)
            rest = rest - term.astype(jnp.float32)
            terms.append(term)
        for term in reversed(terms):
            mix = mix + lax.dot_general(
                match, term, (((0,), (0,)), ((), ())), preferred_element_type=jnp.float32
            )
        for k in range(0, depth, LANES):
            piece = lax.dot_general(
                env, spread[:, k : k + LANES], (((0 if flip else 1,), (0,)), ((), ())),
                preferred_element_type=jnp.float32,
            )
            scaled[c, :, k : k + LANES] = (piece * mix).astype(jnp.bfloat16)

    scale_rows(env_ref[:, :rows], True, 0, 0)

    def split(t):
        unit = lax.div(t, tall)
        return lax.div(unit, CHUNKS), lax.rem(unit, CHUNKS), lax.rem(t, tall)

    def to_mate(t):
        slot = lax.rem(t, RING)
        return pltpu.make_async_remote_copy(
            send_a.at[slot], recv_a.at[slot], sa_sem.at[slot], ra_sem.at[slot],
            device_id={"lbond": mate}, device_id_type=pl.DeviceIdType.MESH,
        )

    def to_across(t):
        slot = lax.rem(t, RING_B)
        return pltpu.make_async_remote_copy(
            send_b.at[slot], recv_b.at[slot], sb_sem.at[slot], rb_sem.at[slot],
            device_id={"lbond": across}, device_id_type=pl.DeviceIdType.MESH,
        )

    def to_owner(site, c, q):
        half = lax.rem(site, 2)
        return pltpu.make_async_remote_copy(
            send_z.at[half, c, q], recv_z.at[half, c, q], sz_sem.at[half, c, q], rz_sem.at[half, c, q],
            device_id={"lbond": at_z(target(q))}, device_id_type=pl.DeviceIdType.MESH,
        )

    pl.semaphore_wait(barrier, len(peers))

    def step(t, carry):
        @pl.when(t < pieces)
        def _():
            site, c, q = split(t)
            goal = target(q)

            @pl.when(c == 0)
            def _():
                n = site * tall + q
                slot = lax.rem(n, 2)
                fetch(n).wait()
                width = packed.shape[-1]
                for b in range(2 * wide):
                    for k in range(0, local, 16):
                        block = raw[slot, k : k + 16, :, b * width : (b + 1) * width]
                        packed[goal, b, k * photon : (k + 16) * photon, :] = block.reshape(16 * photon, width)

                @pl.when(n + 2 < sites * tall)
                def _():
                    fetch(n + 2).start()

            slot = lax.rem(t, RING)
            for b in range(wide):
                send_a[slot, b] = jnp.dot(
                    scaled[c], packed[goal, 2 * b + 1 - core], preferred_element_type=jnp.float32
                ).astype(jnp.bfloat16)
            to_mate(t).start()
            for b in range(wide):
                keep_a[lax.rem(t, 2), b] = jnp.dot(
                    scaled[c], packed[goal, 2 * b + core], preferred_element_type=jnp.float32
                )

        for c in range(1, CHUNKS):
            @pl.when(t == c * tall - 1)
            def _():
                scale_rows(env_ref[:, c * rows : (c + 1) * rows], True, 0, c)

        @pl.when((t >= 1) & (t < pieces + 1))
        def _():
            u = t - 1
            slot = lax.rem(u, RING)
            half = lax.rem(u, 2)
            to_mate(u).wait()
            if wide > 1:
                far = wide - 1 - y
                send_b[lax.rem(u, RING_B)] = (keep_a[half, far] + recv_a[slot, far].astype(jnp.float32)).astype(jnp.bfloat16)
                to_across(u).start()
            keep_b[lax.rem(u, HOLD)] = keep_a[half, y] + recv_a[slot, y].astype(jnp.float32)

        @pl.when((t >= HOLD) & (t < pieces + HOLD))
        def _():
            u = t - HOLD
            site, c, q = split(u)
            total = keep_b[lax.rem(u, HOLD)]
            if wide > 1:
                to_across(u).wait()
                total = total + recv_b[lax.rem(u, RING_B)].astype(jnp.float32)

            @pl.when(q < tall - 1)
            def _():
                send_z[lax.rem(site, 2), c, q] = total.astype(jnp.bfloat16)
                to_owner(site, c, q).start()

            @pl.when(q == tall - 1)
            def _():
                keep_z[c] = total

        last = t - HOLD - LAG

        @pl.when((last >= 0) & (lax.rem(last + 1, tall) == 0))
        def _():
            site, c, _ = split(last)
            total = keep_z[c]
            for q in range(tall - 1):
                to_owner(site, c, q).wait()
                total = total + recv_z[lax.rem(site, 2), c, q].astype(jnp.float32)
            env = (total * (rescale_ref[site].astype(jnp.float32) * 0.5)).astype(jnp.bfloat16)

            @pl.when(site < sites - 1)
            def _():
                scale_rows(env, False, site + 1, c)

            @pl.when(site == sites - 1)
            def _():
                out_ref[pl.ds(pl.multiple_of(c * rows, rows), rows), :] = env

        return carry

    lax.fori_loop(0, pieces + HOLD + LAG, step, 0)


def on_device(wide, tall, env_in, site_tensors, weight_table, state_codes, rescale):
    sites, local, photon, right = site_tensors.shape
    rows = env_in.shape[1] // CHUNKS
    depth = local * photon
    table = jnp.tile(weight_table, (1, LANES // photon))
    vmem = pl.BlockSpec(memory_space=pltpu.VMEM)
    half, full = jnp.bfloat16, jnp.float32
    dma = pltpu.SemaphoreType.DMA
    out = pl.pallas_call(
        functools.partial(kernel, wide, tall),
        out_shape=jax.ShapeDtypeStruct((env_in.shape[1], local), half),
        in_specs=[pl.BlockSpec(memory_space=pltpu.SMEM), vmem, vmem, vmem, pl.BlockSpec(memory_space=pl.ANY)],
        out_specs=vmem,
        scratch_shapes=[
            pltpu.VMEM((2, local, photon, right // tall), half),
            pltpu.VMEM((tall, 2 * wide, depth, local), half),
            pltpu.VMEM((local, depth), half),
            pltpu.VMEM((CHUNKS, rows, depth), half),
            pltpu.VMEM((RING, wide, rows, local), half),
            pltpu.VMEM((RING, wide, rows, local), half),
            pltpu.VMEM((2, wide, rows, local), full),
            pltpu.VMEM((RING_B, rows, local), half),
            pltpu.VMEM((RING_B, rows, local), half),
            pltpu.VMEM((HOLD, rows, local), full),
            pltpu.VMEM((2, CHUNKS, tall - 1, rows, local), half),
            pltpu.VMEM((2, CHUNKS, tall - 1, rows, local), half),
            pltpu.VMEM((CHUNKS, rows, local), full),
            dma((2,)),
            dma((RING,)),
            dma((RING,)),
            dma((RING_B,)),
            dma((RING_B,)),
            dma((2, CHUNKS, tall - 1)),
            dma((2, CHUNKS, tall - 1)),
        ],
        compiler_params=pltpu.CompilerParams(
            collective_id=0, has_side_effects=True, vmem_limit_bytes=60 * 1024 * 1024
        ),
    )(rescale, env_in, state_codes, table, site_tensors)
    return out.T


def solution(mesh):
    wide = max(1, 4 // mesh.shape["groups"])
    tall = mesh.shape["lbond"] // (2 * wide)
    placed = (P("lbond", "groups"), P(None, "lbond", None, None), P(), P(None, "groups"), P())
    return jax.shard_map(
        functools.partial(on_device, wide, tall),
        mesh=mesh, in_specs=placed, out_specs=P("lbond", "groups"), check_vma=False,
    )
```

```python
import functools

import jax
import jax.numpy as jnp
from jax import lax
from jax.experimental import pallas as pl
from jax.experimental.pallas import tpu as pltpu
from jax.sharding import PartitionSpec as P

CHUNKS = 4
HELD_A = 1
HELD_B = 4
LAG = 4
RING_A = 2 * HELD_A + 2
RING_B = 2 * (HELD_B - HELD_A) + 2
LANES = 128


def kernel(
    wide, tall, rescale_ref, env_ref, code_ref, table_ref, tensor_ref, out_ref,
    raw, packed, spread, scaled, send_a, recv_a, keep_a, send_b, recv_b, keep_b,
    send_z, recv_z, keep_z, raw_sem, sa_sem, ra_sem, sb_sem, rb_sem, sz_sem, rz_sem,
):
    sites, local, photon, _ = tensor_ref.shape
    rows = env_ref.shape[1] // CHUNKS
    depth = local * photon
    pieces = sites * CHUNKS * tall
    me = lax.axis_index("lbond")
    core = lax.rem(me, 2)
    chip = lax.div(me, 2)
    y = lax.rem(chip, wide)
    z = lax.div(chip, wide)
    mate = me + 1 - 2 * core
    across = (z * wide + (wide - 1 - y)) * 2 + core

    def at_z(other):
        return (other * wide + y) * 2 + core

    def target(q):
        return lax.rem(z + 1 + q, tall)

    barrier = pltpu.get_barrier_semaphore()
    peers = [mate] + ([across] if wide > 1 else [])
    peers += [at_z(target(q)) for q in range(tall - 1)]
    for peer in peers:
        pl.semaphore_signal(barrier, inc=1, device_id={"lbond": peer}, device_id_type=pl.DeviceIdType.MESH)

    def fetch(n):
        site = lax.div(n, tall)
        goal = target(lax.rem(n, tall))
        width = raw.shape[-1]
        columns = pl.ds(pl.multiple_of(goal * width, LANES), width)
        slot = lax.rem(n, 2)
        return pltpu.make_async_copy(tensor_ref.at[site, :, :, columns], raw.at[slot], raw_sem.at[slot])

    for n in range(2):
        fetch(jnp.int32(n)).start()

    left = lax.broadcasted_iota(jnp.int32, (local, depth), 0)
    flat = lax.broadcasted_iota(jnp.int32, (local, depth), 1)
    spread[...] = jnp.where(
        (flat >= left * photon) & (flat < left * photon + photon), 1.0, 0.0
    ).astype(jnp.bfloat16)

    def scale_rows(env, flip, site, c):
        line = code_ref[pl.ds(site, 1), :]
        codes = line[:, :rows]
        for k in range(1, CHUNKS):
            codes = jnp.where(c == k, line[:, k * rows : (k + 1) * rows], codes)
        entries = table_ref.shape[0]
        index = lax.broadcasted_iota(jnp.int32, (entries, rows), 0)
        match = jnp.where(index == codes, 1.0, 0.0).astype(jnp.bfloat16)
        mix = jnp.zeros((rows, LANES), jnp.float32)
        rest = table_ref[...]
        terms = []
        for _ in range(3):
            term = rest.astype(jnp.bfloat16)
            rest = rest - term.astype(jnp.float32)
            terms.append(term)
        for term in reversed(terms):
            mix = mix + lax.dot_general(
                match, term, (((0,), (0,)), ((), ())), preferred_element_type=jnp.float32
            )
        for k in range(0, depth, LANES):
            piece = lax.dot_general(
                env, spread[:, k : k + LANES], (((0 if flip else 1,), (0,)), ((), ())),
                preferred_element_type=jnp.float32,
            )
            scaled[c, :, k : k + LANES] = (piece * mix).astype(jnp.bfloat16)

    scale_rows(env_ref[:, :rows], True, 0, 0)

    def split(t):
        unit = lax.div(t, tall)
        return lax.div(unit, CHUNKS), lax.rem(unit, CHUNKS), lax.rem(t, tall)

    def to_mate(t):
        slot = lax.rem(t, RING_A)
        return pltpu.make_async_remote_copy(
            send_a.at[slot], recv_a.at[slot], sa_sem.at[slot], ra_sem.at[slot],
            device_id={"lbond": mate}, device_id_type=pl.DeviceIdType.MESH,
        )

    def to_across(t):
        slot = lax.rem(t, RING_B)
        return pltpu.make_async_remote_copy(
            send_b.at[slot], recv_b.at[slot], sb_sem.at[slot], rb_sem.at[slot],
            device_id={"lbond": across}, device_id_type=pl.DeviceIdType.MESH,
        )

    def to_owner(site, c, q):
        half = lax.rem(site, 2)
        return pltpu.make_async_remote_copy(
            send_z.at[half, c, q], recv_z.at[half, c, q], sz_sem.at[half, c, q], rz_sem.at[half, c, q],
            device_id={"lbond": at_z(target(q))}, device_id_type=pl.DeviceIdType.MESH,
        )

    pl.semaphore_wait(barrier, len(peers))

    def step(t, carry):
        @pl.when(t < pieces)
        def _():
            site, c, q = split(t)
            goal = target(q)

            @pl.when(c == 0)
            def _():
                n = site * tall + q
                slot = lax.rem(n, 2)
                fetch(n).wait()
                width = packed.shape[-1]
                for b in range(2 * wide):
                    for k in range(0, local, 16):
                        block = raw[slot, k : k + 16, :, b * width : (b + 1) * width]
                        packed[goal, b, k * photon : (k + 16) * photon, :] = block.reshape(16 * photon, width)

                @pl.when(n + 2 < sites * tall)
                def _():
                    fetch(n + 2).start()

            slot = lax.rem(t, RING_A)
            for b in range(wide):
                send_a[slot, b] = jnp.dot(
                    scaled[c], packed[goal, 2 * b + 1 - core], preferred_element_type=jnp.float32
                ).astype(jnp.bfloat16)
            to_mate(t).start()
            for b in range(wide):
                keep_a[lax.rem(t, HELD_A + 1), b] = jnp.dot(
                    scaled[c], packed[goal, 2 * b + core], preferred_element_type=jnp.float32
                )

        for c in range(1, CHUNKS):
            @pl.when(t == c * tall - 1)
            def _():
                scale_rows(env_ref[:, c * rows : (c + 1) * rows], True, 0, c)

        @pl.when((t >= HELD_A) & (t < pieces + HELD_A))
        def _():
            u = t - HELD_A
            slot = lax.rem(u, RING_A)
            half = lax.rem(u, HELD_A + 1)
            to_mate(u).wait()
            if wide > 1:
                far = wide - 1 - y
                send_b[lax.rem(u, RING_B)] = (keep_a[half, far] + recv_a[slot, far].astype(jnp.float32)).astype(jnp.bfloat16)
                to_across(u).start()
            keep_b[lax.rem(u, HELD_B - HELD_A + 1)] = keep_a[half, y] + recv_a[slot, y].astype(jnp.float32)

        @pl.when((t >= HELD_B) & (t < pieces + HELD_B))
        def _():
            u = t - HELD_B
            site, c, q = split(u)
            total = keep_b[lax.rem(u, HELD_B - HELD_A + 1)]
            if wide > 1:
                to_across(u).wait()
                total = total + recv_b[lax.rem(u, RING_B)].astype(jnp.float32)

            @pl.when(q < tall - 1)
            def _():
                send_z[lax.rem(site, 2), c, q] = total.astype(jnp.bfloat16)
                to_owner(site, c, q).start()

            @pl.when(q == tall - 1)
            def _():
                keep_z[c] = total

        last = t - HELD_B - LAG

        @pl.when((last >= 0) & (lax.rem(last + 1, tall) == 0))
        def _():
            site, c, _ = split(last)
            total = keep_z[c]
            for q in range(tall - 1):
                to_owner(site, c, q).wait()
                total = total + recv_z[lax.rem(site, 2), c, q].astype(jnp.float32)
            env = (total * (rescale_ref[site].astype(jnp.float32) * 0.5)).astype(jnp.bfloat16)

            @pl.when(site < sites - 1)
            def _():
                scale_rows(env, False, site + 1, c)

            @pl.when(site == sites - 1)
            def _():
                out_ref[pl.ds(pl.multiple_of(c * rows, rows), rows), :] = env

        return carry

    lax.fori_loop(0, pieces + HELD_B + LAG, step, 0)


def on_device(wide, tall, env_in, site_tensors, weight_table, state_codes, rescale):
    sites, local, photon, right = site_tensors.shape
    rows = env_in.shape[1] // CHUNKS
    depth = local * photon
    table = jnp.tile(weight_table, (1, LANES // photon))
    vmem = pl.BlockSpec(memory_space=pltpu.VMEM)
    half, full = jnp.bfloat16, jnp.float32
    dma = pltpu.SemaphoreType.DMA
    out = pl.pallas_call(
        functools.partial(kernel, wide, tall),
        out_shape=jax.ShapeDtypeStruct((env_in.shape[1], local), half),
        in_specs=[pl.BlockSpec(memory_space=pltpu.SMEM), vmem, vmem, vmem, pl.BlockSpec(memory_space=pl.ANY)],
        out_specs=vmem,
        scratch_shapes=[
            pltpu.VMEM((2, local, photon, right // tall), half),
            pltpu.VMEM((tall, 2 * wide, depth, local), half),
            pltpu.VMEM((local, depth), half),
            pltpu.VMEM((CHUNKS, rows, depth), half),
            pltpu.VMEM((RING_A, wide, rows, local), half),
            pltpu.VMEM((RING_A, wide, rows, local), half),
            pltpu.VMEM((HELD_A + 1, wide, rows, local), full),
            pltpu.VMEM((RING_B, rows, local), half),
            pltpu.VMEM((RING_B, rows, local), half),
            pltpu.VMEM((HELD_B - HELD_A + 1, rows, local), full),
            pltpu.VMEM((2, CHUNKS, tall - 1, rows, local), half),
            pltpu.VMEM((2, CHUNKS, tall - 1, rows, local), half),
            pltpu.VMEM((CHUNKS, rows, local), full),
            dma((2,)),
            dma((RING_A,)),
            dma((RING_A,)),
            dma((RING_B,)),
            dma((RING_B,)),
            dma((2, CHUNKS, tall - 1)),
            dma((2, CHUNKS, tall - 1)),
        ],
        compiler_params=pltpu.CompilerParams(
            collective_id=0, has_side_effects=True, vmem_limit_bytes=60 * 1024 * 1024
        ),
    )(rescale, env_in, state_codes, table, site_tensors)
    return out.T


def solution(mesh):
    wide = max(1, 4 // mesh.shape["groups"])
    tall = mesh.shape["lbond"] // (2 * wide)
    placed = (P("lbond", "groups"), P(None, "lbond", None, None), P(), P(None, "groups"), P())
    return jax.shard_map(
        functools.partial(on_device, wide, tall),
        mesh=mesh, in_specs=placed, out_specs=P("lbond", "groups"), check_vma=False,
    )
```

```python
import functools

import jax
import jax.numpy as jnp
from jax import lax
from jax.experimental import pallas as pl
from jax.experimental.pallas import tpu as pltpu
from jax.sharding import PartitionSpec as P

CHUNKS = 4
HELD_A = 1
HELD_B = 4
LAG = 4
RING_A = 2 * HELD_A + 2
RING_B = 2 * (HELD_B - HELD_A) + 2
LANES = 128


def kernel(
    wide, tall, rescale_ref, env_ref, code_ref, table_ref, tensor_ref, out_ref,
    raw, packed, spread, scaled, send_a, recv_a, keep_a, send_b, recv_b, keep_b,
    send_z, recv_z, keep_z, raw_sem, sa_sem, ra_sem, sb_sem, rb_sem, sz_sem, rz_sem,
):
    sites, local, photon, _ = tensor_ref.shape
    rows = env_ref.shape[1] // CHUNKS
    depth = local * photon
    pieces = sites * CHUNKS * tall
    me = lax.axis_index("lbond")
    core = lax.rem(me, 2)
    chip = lax.div(me, 2)
    y = lax.rem(chip, wide)
    z = lax.div(chip, wide)
    mate = me + 1 - 2 * core
    across = (z * wide + (wide - 1 - y)) * 2 + core

    def at_z(other):
        return (other * wide + y) * 2 + core

    def target(q):
        return lax.rem(z + 1 + q, tall)

    barrier = pltpu.get_barrier_semaphore()
    peers = [mate] + ([across] if wide > 1 else [])
    peers += [at_z(target(q)) for q in range(tall - 1)]
    for peer in peers:
        pl.semaphore_signal(barrier, inc=1, device_id={"lbond": peer}, device_id_type=pl.DeviceIdType.MESH)

    def fetch(n):
        site = lax.div(n, tall)
        goal = target(lax.rem(n, tall))
        width = raw.shape[-1]
        columns = pl.ds(pl.multiple_of(goal * width, LANES), width)
        slot = lax.rem(n, 2)
        return pltpu.make_async_copy(tensor_ref.at[site, :, :, columns], raw.at[slot], raw_sem.at[slot])

    for n in range(2):
        fetch(jnp.int32(n)).start()

    left = lax.broadcasted_iota(jnp.int32, (local, depth), 0)
    flat = lax.broadcasted_iota(jnp.int32, (local, depth), 1)
    spread[...] = jnp.where(
        (flat >= left * photon) & (flat < left * photon + photon), 1.0, 0.0
    ).astype(jnp.bfloat16)

    def scale_rows(env, flip, site, c):
        line = code_ref[pl.ds(site, 1), :]
        codes = line[:, :rows]
        for k in range(1, CHUNKS):
            codes = jnp.where(c == k, line[:, k * rows : (k + 1) * rows], codes)
        entries = table_ref.shape[0]
        index = lax.broadcasted_iota(jnp.int32, (entries, rows), 0)
        match = jnp.where(index == codes, 1.0, 0.0).astype(jnp.bfloat16)
        mix = jnp.zeros((rows, LANES), jnp.float32)
        rest = table_ref[...]
        terms = []
        for _ in range(3):
            term = rest.astype(jnp.bfloat16)
            rest = rest - term.astype(jnp.float32)
            terms.append(term)
        for term in reversed(terms):
            mix = mix + lax.dot_general(
                match, term, (((0,), (0,)), ((), ())), preferred_element_type=jnp.float32
            )
        for k in range(0, depth, LANES):
            piece = lax.dot_general(
                env, spread[:, k : k + LANES], (((0 if flip else 1,), (0,)), ((), ())),
                preferred_element_type=jnp.float32,
            )
            scaled[c, :, k : k + LANES] = (piece * mix).astype(jnp.bfloat16)

    scale_rows(env_ref[:, :rows], True, 0, 0)

    def split(t):
        unit = lax.div(t, tall)
        return lax.div(unit, CHUNKS), lax.rem(unit, CHUNKS), lax.rem(t, tall)

    def to_mate(t):
        slot = lax.rem(t, RING_A)
        return pltpu.make_async_remote_copy(
            send_a.at[slot], recv_a.at[slot], sa_sem.at[slot], ra_sem.at[slot],
            device_id={"lbond": mate}, device_id_type=pl.DeviceIdType.MESH,
        )

    def to_across(t):
        slot = lax.rem(t, RING_B)
        return pltpu.make_async_remote_copy(
            send_b.at[slot], recv_b.at[slot], sb_sem.at[slot], rb_sem.at[slot],
            device_id={"lbond": across}, device_id_type=pl.DeviceIdType.MESH,
        )

    def to_owner(site, c, q):
        half = lax.rem(site, 2)
        return pltpu.make_async_remote_copy(
            send_z.at[half, c, q], recv_z.at[half, c, q], sz_sem.at[half, c, q], rz_sem.at[half, c, q],
            device_id={"lbond": at_z(target(q))}, device_id_type=pl.DeviceIdType.MESH,
        )

    pl.semaphore_wait(barrier, len(peers))


    def repack(n, goal, which):
        slot = lax.rem(n, 2)
        width = packed.shape[-1]
        for b in range(wide):
            part = 2 * b + which
            lanes = pl.ds(pl.multiple_of(part * width, LANES), width)
            for k in range(0, local, 16):
                block = raw[slot, k : k + 16, :, lanes]
                packed[goal, part, k * photon : (k + 16) * photon, :] = block.reshape(16 * photon, width)

    def step(t, carry):
        @pl.when(t < pieces)
        def _():
            site, c, q = split(t)
            goal = target(q)

            @pl.when(c == 0)
            def _():
                n = site * tall + q
                fetch(n).wait()
                repack(n, goal, 1 - core)


            slot = lax.rem(t, RING_A)
            for b in range(wide):
                send_a[slot, b] = jnp.dot(
                    scaled[c], packed[goal, 2 * b + 1 - core], preferred_element_type=jnp.float32
                ).astype(jnp.bfloat16)
            to_mate(t).start()

            @pl.when(c == 0)
            def _():
                n = site * tall + q
                repack(n, goal, core)

                @pl.when(n + 2 < sites * tall)
                def _():
                    fetch(n + 2).start()

            for b in range(wide):
                keep_a[lax.rem(t, HELD_A + 1), b] = jnp.dot(
                    scaled[c], packed[goal, 2 * b + core], preferred_element_type=jnp.float32
                )

        for c in range(1, CHUNKS):
            @pl.when(t == c * tall - 1)
            def _():
                scale_rows(env_ref[:, c * rows : (c + 1) * rows], True, 0, c)

        @pl.when((t >= HELD_A) & (t < pieces + HELD_A))
        def _():
            u = t - HELD_A
            slot = lax.rem(u, RING_A)
            half = lax.rem(u, HELD_A + 1)
            to_mate(u).wait()
            if wide > 1:
                far = wide - 1 - y
                send_b[lax.rem(u, RING_B)] = (keep_a[half, far] + recv_a[slot, far].astype(jnp.float32)).astype(jnp.bfloat16)
                to_across(u).start()
            keep_b[lax.rem(u, HELD_B - HELD_A + 1)] = keep_a[half, y] + recv_a[slot, y].astype(jnp.float32)

        @pl.when((t >= HELD_B) & (t < pieces + HELD_B))
        def _():
            u = t - HELD_B
            site, c, q = split(u)
            total = keep_b[lax.rem(u, HELD_B - HELD_A + 1)]
            if wide > 1:
                to_across(u).wait()
                total = total + recv_b[lax.rem(u, RING_B)].astype(jnp.float32)

            @pl.when(q < tall - 1)
            def _():
                send_z[lax.rem(site, 2), c, q] = total.astype(jnp.bfloat16)
                to_owner(site, c, q).start()

            @pl.when(q == tall - 1)
            def _():
                keep_z[c] = total

        last = t - HELD_B - LAG

        @pl.when((last >= 0) & (lax.rem(last + 1, tall) == 0))
        def _():
            site, c, _ = split(last)
            total = keep_z[c]
            for q in range(tall - 1):
                to_owner(site, c, q).wait()
                total = total + recv_z[lax.rem(site, 2), c, q].astype(jnp.float32)
            env = (total * (rescale_ref[site].astype(jnp.float32) * 0.5)).astype(jnp.bfloat16)

            @pl.when(site < sites - 1)
            def _():
                scale_rows(env, False, site + 1, c)

            @pl.when(site == sites - 1)
            def _():
                out_ref[:, pl.ds(pl.multiple_of(c * rows, rows), rows)] = jnp.transpose(env)

        return carry

    lax.fori_loop(0, pieces + HELD_B + LAG, step, 0)


def on_device(wide, tall, env_in, site_tensors, weight_table, state_codes, rescale):
    sites, local, photon, right = site_tensors.shape
    rows = env_in.shape[1] // CHUNKS
    depth = local * photon
    table = jnp.tile(weight_table, (1, LANES // photon))
    vmem = pl.BlockSpec(memory_space=pltpu.VMEM)
    half, full = jnp.bfloat16, jnp.float32
    dma = pltpu.SemaphoreType.DMA
    out = pl.pallas_call(
        functools.partial(kernel, wide, tall),
        out_shape=jax.ShapeDtypeStruct((local, env_in.shape[1]), half),
        in_specs=[pl.BlockSpec(memory_space=pltpu.SMEM), vmem, vmem, vmem, pl.BlockSpec(memory_space=pl.ANY)],
        out_specs=vmem,
        scratch_shapes=[
            pltpu.VMEM((2, local, photon, right // tall), half),
            pltpu.VMEM((tall, 2 * wide, depth, local), half),
            pltpu.VMEM((local, depth), half),
            pltpu.VMEM((CHUNKS, rows, depth), half),
            pltpu.VMEM((RING_A, wide, rows, local), half),
            pltpu.VMEM((RING_A, wide, rows, local), half),
            pltpu.VMEM((HELD_A + 1, wide, rows, local), full),
            pltpu.VMEM((RING_B, rows, local), half),
            pltpu.VMEM((RING_B, rows, local), half),
            pltpu.VMEM((HELD_B - HELD_A + 1, rows, local), full),
            pltpu.VMEM((2, CHUNKS, tall - 1, rows, local), half),
            pltpu.VMEM((2, CHUNKS, tall - 1, rows, local), half),
            pltpu.VMEM((CHUNKS, rows, local), full),
            dma((2,)),
            dma((RING_A,)),
            dma((RING_A,)),
            dma((RING_B,)),
            dma((RING_B,)),
            dma((2, CHUNKS, tall - 1)),
            dma((2, CHUNKS, tall - 1)),
        ],
        compiler_params=pltpu.CompilerParams(
            collective_id=0, has_side_effects=True, vmem_limit_bytes=60 * 1024 * 1024
        ),
    )(rescale, env_in, state_codes, table, site_tensors)
    return out


def solution(mesh):
    wide = max(1, 4 // mesh.shape["groups"])
    tall = mesh.shape["lbond"] // (2 * wide)
    placed = (P("lbond", "groups"), P(None, "lbond", None, None), P(), P(None, "groups"), P())
    return jax.shard_map(
        functools.partial(on_device, wide, tall),
        mesh=mesh, in_specs=placed, out_specs=P("lbond", "groups"), check_vma=False,
    )
```
